768 devices in a mesh: section: 24 (over z_lo, x, core), seq: 32 (over z_hi, y).
Axes of the slice: x: 4, y: 8, z: 12 (z_hi: 4, z_lo: 3; z = z_hi * 3 + z_lo), core: 2. Of those that a mesh axis runs over, the one named last changes fastest.
Arguments:
- queries: bfloat16 [8192, 3072], P('seq', 'section'), may hold values from -64 to 64
- key_rows: bfloat16 [8192, 3072], P('seq', 'section'), may hold values from -64 to 64
- values: bfloat16 [8192, 3072], P('seq', 'section'), may hold values from -6 to 6
- out_grad: bfloat16 [8192, 3072], P('seq', 'section'), may hold values from -6 to 6
- query_gain: float32 [3072], P('section'), may hold values from 1 to 3
- key_gain: float32 [3072], P('section'), may hold values from 1 to 3
- stretch_id: int32 [8192], P('seq'), may hold values from 0 to 31, as said below
Outputs:
- attended: bfloat16 [8192, 3072], P('seq', 'section')
- grad_queries: float32 [8192, 3072], P('seq', 'section')
- grad_keys: float32 [8192, 3072], P('seq', 'section')
- grad_values: float32 [8192, 3072], P('seq', 'section')
The draws below stay inside these ranges and needn't reach their ends.
Inputs may be any that keep to these rules, and one draw needn't show every extreme that they name: stretch_id never falls along the tokens and changes only at multiples of 128 tokens (whole latent frames); the first frame is stretch 0 alone, stretch 1 spans exactly three frames (384 tokens); from frame 4 on, stretches come in consecutive pairs that together span exactly four frames, each stretch one to three frames.
All inputs are finite; a program needn't handle non-finite values.
Results may differ from the reference program's by a relative error of at most 0.038.
Values may be sent and summed in bfloat16 or wider, within the bound.
No kernel may reach another device: no remote copies, remote signals or barrier semaphores. Data moves between devices by JAX's collectives and lax.ppermute only.
A program may use at most 32 MiB of HBM per device.

```python
import math
import jax
import jax.numpy as jnp
from jax import lax

HEAD_DIM = 128
TOK_DEV = 256
HEADS = 24
WIDTH = 3072
TOKENS = 8192
FRAME_TOK = 128
N_SEQ = 32


def pair_draw(key):
    width = HEADS * HEAD_DIM
    streams = jax.random.split(key, 5)
    head_of = (jnp.arange(width) // HEAD_DIM).astype(jnp.float32)
    column_scale = jnp.exp(jax.random.uniform(streams[0], (width,), jnp.float32, math.log(0.3), math.log(3.0)))
    query_scale = jnp.exp(jax.random.uniform(streams[1], (TOKENS, 1), jnp.float32, math.log(0.3), math.log(3.0)))
    key_scale = jnp.exp(jax.random.uniform(streams[2], (TOKENS, 1), jnp.float32, math.log(0.3), math.log(3.0)))
    spread = max(HEADS - 1, 1)
    ramp = math.sqrt(3.0) ** (head_of / spread)
    query_base = jnp.clip(jax.random.normal(streams[3], (TOKENS, width), jnp.float32), -4.0, 4.0)
    key_base = jnp.clip(jax.random.normal(streams[4], (TOKENS, width), jnp.float32), -4.0, 4.0)
    query_draw = query_base * column_scale[None, :] * ramp[None, :] * query_scale
    key_draw = key_base * column_scale[None, :] * ramp[None, :] * key_scale
    return (jnp.clip(query_draw, -64.0, 64.0), jnp.clip(key_draw, -64.0, 64.0))


def draw_queries(key, part):
    return pair_draw(jax.random.fold_in(key, 7))[0].astype(jnp.bfloat16)


def draw_key_rows(key, part):
    return pair_draw(jax.random.fold_in(key, 7))[1].astype(jnp.bfloat16)


def draw_stretch_id(key, part):
    frame_count = TOKENS // FRAME_TOK
    group_count = (frame_count - 4) // 4
    picks = jax.random.randint(jax.random.fold_in(key, 11), (group_count,), 0, 3).astype(jnp.int32)
    first_span = (picks + 1).astype(jnp.int32)
    second_span = (4 - first_span).astype(jnp.int32)
    paired = jnp.stack([first_span, second_span], axis=1).reshape(2 * group_count)
    spans = jnp.concatenate([jnp.array([1, 3], jnp.int32), paired.astype(jnp.int32)])
    starts = jnp.cumsum(spans) - spans
    frame_of = (jnp.arange(TOKENS, dtype=jnp.int32) // FRAME_TOK).astype(jnp.int32)
    stretch = jnp.sum((starts[None, :] <= frame_of[:, None]).astype(jnp.int32), axis=1) - 1
    return stretch.astype(jnp.int32)


def level_of(key, shape, shards, smallest, top_value):
    level = 1.0
    for axis_at, shards_of in shards:
        draws = jax.random.uniform(jax.random.fold_in(jax.random.fold_in(key, 6), axis_at), (shards_of,), jnp.float32, smallest / len(shards), top_value / len(shards))
        level = level * jnp.repeat(jnp.exp(draws), shape[axis_at] // shards_of).reshape((-1,) + (1,) * (len(shape) - 1 - axis_at))
    return level


def bell_draw(own_key, dims, scale, limit, shards=(), kind=jnp.bfloat16):
    level = level_of(own_key, dims, shards, -0.22, 0.18) if shards else 1.0
    result = jax.random.normal(own_key, dims, jnp.float32) * scale * level
    return jnp.minimum(jnp.maximum(result, -limit), limit).astype(kind)


def setup_inputs(seed: int = 0) -> dict:
    streams_of = jax.random.split(jax.random.key(seed), 8)
    queries = draw_queries(jax.random.fold_in(streams_of[7], 71), 0)
    key_rows = draw_key_rows(jax.random.fold_in(streams_of[7], 71), 0)
    values = bell_draw(streams_of[2], (TOKENS, WIDTH), 1.0, 6.0, ((0, 32), (1, 24)))
    out_grad = bell_draw(streams_of[3], (TOKENS, WIDTH), 1.0, 6.0, ((0, 32), (1, 24)))
    query_gain = jnp.clip(1.0 + 2.0 * jax.random.uniform(streams_of[4], (WIDTH,), jnp.float32) ** level_of(streams_of[4], (WIDTH,), ((0, 24),), -0.2, 0.2), 1.0, 3.0)
    key_gain = jnp.clip(1.0 + 2.0 * jax.random.uniform(streams_of[5], (WIDTH,), jnp.float32) ** level_of(streams_of[5], (WIDTH,), ((0, 24),), -0.2, 0.2), 1.0, 3.0)
    stretch_id = draw_stretch_id(jax.random.fold_in(streams_of[7], 71), 0)
    return {"queries": queries, "key_rows": key_rows, "values": values, "out_grad": out_grad, "query_gain": query_gain, "key_gain": key_gain, "stretch_id": stretch_id}


EPSILON = 1e-06

def normalize(raw_rows, gain):
    widened = raw_rows.astype(jnp.float32)
    inv_root = lax.rsqrt(lax.optimization_barrier(jnp.mean(widened * widened, axis=1)) + EPSILON)
    normed = (widened * inv_root[:, None] * gain[None, :]).astype(jnp.bfloat16)
    return (widened, inv_root, normed)

def norm_backward(widened, inv_root, gain, grad_hat):
    row_term = lax.optimization_barrier(jnp.sum(grad_hat * gain[None, :] * widened, axis=1))
    return gain[None, :] * inv_root[:, None] * grad_hat - widened * (inv_root ** 3 * row_term / WIDTH)[:, None]

def head_split(matrix):
    return jnp.transpose(matrix.reshape(TOKENS, HEADS, HEAD_DIM), (1, 0, 2))

def head_merge(stacked):
    return jnp.transpose(stacked, (1, 0, 2)).reshape(TOKENS, WIDTH)

def one_head(operands, stretch_id):
    query_hat, key_hat, value_rows, grad_rows = operands
    score_scale = 1.0 / math.sqrt(HEAD_DIM)
    blocked = (query_hat.reshape(N_SEQ, TOK_DEV, HEAD_DIM), grad_rows.reshape(N_SEQ, TOK_DEV, HEAD_DIM), stretch_id.reshape(N_SEQ, TOK_DEV))

    def block_step(carried, block_rows):
        key_grad, value_grad = carried
        query_block, grad_block, stretch_block = block_rows
        scores = jnp.dot(query_block, key_hat.T, preferred_element_type=jnp.float32) * score_scale
        visible = stretch_id[None, :] <= stretch_block[:, None]
        scores = jnp.where(visible, scores, -jnp.inf)
        row_top = lax.optimization_barrier(jnp.max(scores, axis=1))
        weights = jnp.exp(scores - row_top[:, None])
        row_sum = lax.optimization_barrier(jnp.sum(weights, axis=1))
        attended = (jnp.dot(weights.astype(jnp.bfloat16), value_rows, preferred_element_type=jnp.float32) / row_sum[:, None]).astype(jnp.bfloat16)
        log_total = row_top + jnp.log(row_sum)
        row_delta = lax.optimization_barrier(jnp.sum(grad_block.astype(jnp.float32) * attended.astype(jnp.float32), axis=1))
        chances = jnp.exp(scores - log_total[:, None])
        grad_chances = jnp.dot(grad_block, value_rows.T, preferred_element_type=jnp.float32)
        grad_scores = (chances * (grad_chances - row_delta[:, None])).astype(jnp.bfloat16)
        query_grad = jnp.dot(grad_scores, key_hat, preferred_element_type=jnp.float32) * score_scale
        key_grad = key_grad + jnp.dot(grad_scores.T, query_block, preferred_element_type=jnp.float32) * score_scale
        value_grad = value_grad + jnp.dot(chances.astype(jnp.bfloat16).T, grad_block, preferred_element_type=jnp.float32)
        return ((key_grad, value_grad), (attended, query_grad))
    zero_rows = jnp.zeros((TOKENS, HEAD_DIM), jnp.float32)
    (key_grad, value_grad), (attended, query_grad) = lax.scan(block_step, (zero_rows, zero_rows), blocked)
    return (attended.reshape(TOKENS, HEAD_DIM), query_grad.reshape(TOKENS, HEAD_DIM), key_grad, value_grad)

def reference(queries, key_rows, values, out_grad, query_gain, key_gain, stretch_id):
    query_wide, query_root, query_hat = normalize(queries, query_gain)
    key_wide, key_root, key_hat = normalize(key_rows, key_gain)
    operands = (head_split(query_hat), head_split(key_hat), head_split(values), head_split(out_grad))
    attended, query_grad, key_grad, value_grad = lax.map(lambda parts: one_head(parts, stretch_id), operands)
    grad_queries = norm_backward(query_wide, query_root, query_gain, head_merge(query_grad))
    grad_keys = norm_backward(key_wide, key_root, key_gain, head_merge(key_grad))
    return (head_merge(attended), grad_queries, grad_keys, head_merge(value_grad))
```

```python
import math

import jax
import jax.numpy as jnp
from jax import lax
from jax.experimental import pallas as pl
from jax.experimental.pallas import tpu as pltpu
from jax.sharding import Mesh, PartitionSpec as P

EPSILON = 1e-06
NEG_FILL = -1e30
FLOOR = -1e20
LOG2E = 1.4426950408889634
SECTION = ("z_lo", "x", "core")
SEQ = ("z_hi", "y")
EXTRA = 16
NT = (((1,), (1,)), ((), ()))
NN = (((1,), (0,)), ((), ()))
TN = (((0,), (0,)), ((), ()))


def dot(a, b, dims):
    return lax.dot_general(a, b, dims, preferred_element_type=jnp.float32)


def forward_kernel(zh_ref, qd_ref, kv_ref, sid_ref, p_ref, o_ref, st_ref):
    rows = sid_ref.shape[0]
    dim = o_ref.shape[1]
    groups = kv_ref.shape[0]
    base = LOG2E / math.sqrt(dim)
    zh = zh_ref[0]
    q = qd_ref[0, :rows, :dim]
    do = qd_ref[0, :rows, dim:]
    sid_q = qd_ref[0, rows : rows + EXTRA, :][:1, :].astype(jnp.float32)
    hidden = sid_ref[:, :1] > sid_q

    def run(count):
        parts = []
        top = None
        for b in range(count):
            s = dot(kv_ref[b, :, :dim], q, NT)
            if b == count - 1:
                s = jnp.where(hidden, NEG_FILL, s)
            parts.append(s)
            one = jnp.max(s, axis=0, keepdims=True)
            top = one if top is None else jnp.maximum(top, one)
        top = jnp.maximum(top, FLOOR)
        total = None
        acc = None
        for b in range(count):
            w = jnp.exp2((parts[b] - top) * base)
            one = jnp.sum(w, axis=0, keepdims=True)
            total = one if total is None else total + one
            wb = w.astype(jnp.bfloat16)
            p_ref[0, b] = wb
            out = dot(kv_ref[b, :, dim:], wb, TN)
            acc = out if acc is None else acc + out
        o_ref[0] = acc
        do_t = do.astype(jnp.float32).T
        delta = jnp.sum(acc * do_t, axis=0, keepdims=True)
        safe = jnp.maximum(total, 1e-30)
        st_ref[0, 0:1, :] = top * base + jnp.log2(safe)
        st_ref[0, 1:2, :] = delta / safe
        st_ref[0, 2:3, :] = top * base

    for g in range(groups):
        pl.when(zh == g)(lambda g=g: run(g + 1))


def backward_kernel(zh_ref, qd_ref, kv_ref, p_ref, o_ref, st_ref, all_ref, y_ref, z_ref, dk_ref, dv_ref):
    j = pl.program_id(0)
    rows = z_ref.shape[1]
    dim = o_ref.shape[1]
    groups = kv_ref.shape[0]
    scale = 1.0 / math.sqrt(dim)
    zh = zh_ref[0]

    @pl.when(j == 0)
    def _():
        dk_ref[...] = jnp.zeros_like(dk_ref)
        dv_ref[...] = jnp.zeros_like(dv_ref)

    q = qd_ref[0, :rows, :dim]
    do = qd_ref[0, :rows, dim:]
    lses = all_ref[:, 0, 0, :]
    tops = jnp.max(lses, axis=0, keepdims=True)
    fac = jnp.exp2(lses - tops)
    total = jnp.sum(fac, axis=0, keepdims=True)
    delta = jnp.sum(fac * all_ref[:, 0, 1, :], axis=0, keepdims=True) / total
    lse = tops + jnp.log2(total)
    c = jnp.exp2(st_ref[0, 2:3, :] - lse)
    y_ref[0, :dim, :] = (o_ref[0] * c).astype(jnp.bfloat16)

    def run(count):
        acc = None
        for b in range(count):
            k = kv_ref[b, :, :dim]
            dp = dot(kv_ref[b, :, dim:], do, NT)
            chance = p_ref[0, b].astype(jnp.float32) * c
            ds = (chance * (dp - delta)).astype(jnp.bfloat16)
            dv_ref[b] += dot(chance.astype(jnp.bfloat16), do, NN)
            dk_ref[b] += dot(ds, q, NN)
            out = dot(k, ds, TN)
            acc = out if acc is None else acc + out
        y_ref[0, dim:, :] = (acc * scale).astype(jnp.bfloat16)

    for g in range(groups):
        pl.when(zh == g)(lambda g=g: run(g + 1))

    @pl.when(j == pl.num_programs(0) - 1)
    def _():
        z_ref[:, :, :dim] = (dk_ref[...] * scale).astype(jnp.bfloat16)
        z_ref[:, :, dim:] = dv_ref[...].astype(jnp.bfloat16)


def forward(zh, qd, kv, sid):
    ny, packed, wide = qd.shape
    nz, rows, _ = kv.shape
    dim = wide // 2
    flops = 2 * 2 * ny * rows * nz * rows * dim
    return pl.pallas_call(
        forward_kernel,
        grid_spec=pltpu.PrefetchScalarGridSpec(
            num_scalar_prefetch=1,
            grid=(ny,),
            in_specs=[
                pl.BlockSpec((1, packed, wide), lambda j, z: (j, 0, 0)),
                pl.BlockSpec((nz, rows, wide), lambda j, z: (0, 0, 0)),
                pl.BlockSpec((rows, 128), lambda j, z: (0, 0)),
            ],
            out_specs=[
                pl.BlockSpec((1, nz, rows, rows), lambda j, z: (j, 0, 0, 0)),
                pl.BlockSpec((1, dim, rows), lambda j, z: (j, 0, 0)),
                pl.BlockSpec((1, 8, rows), lambda j, z: (j, 0, 0)),
            ],
        ),
        out_shape=[
            jax.ShapeDtypeStruct((ny, nz, rows, rows), jnp.bfloat16),
            jax.ShapeDtypeStruct((ny, dim, rows), jnp.float32),
            jax.ShapeDtypeStruct((ny, 8, rows), jnp.float32),
        ],
        cost_estimate=pl.CostEstimate(flops=flops, transcendentals=ny * nz * rows * rows, bytes_accessed=8 << 20),
        name="attend",
    )(zh, qd, kv, sid)


def backward(zh, qd, kv, p, o, st, all_st):
    ny, packed, wide = qd.shape
    nz, rows, _ = kv.shape
    dim = wide // 2
    flops = 4 * 2 * ny * rows * nz * rows * dim
    return pl.pallas_call(
        backward_kernel,
        grid_spec=pltpu.PrefetchScalarGridSpec(
            num_scalar_prefetch=1,
            grid=(ny,),
            in_specs=[
                pl.BlockSpec((1, packed, wide), lambda j, z: (j, 0, 0)),
                pl.BlockSpec((nz, rows, wide), lambda j, z: (0, 0, 0)),
                pl.BlockSpec((1, nz, rows, rows), lambda j, z: (j, 0, 0, 0)),
                pl.BlockSpec((1, dim, rows), lambda j, z: (j, 0, 0)),
                pl.BlockSpec((1, 8, rows), lambda j, z: (j, 0, 0)),
                pl.BlockSpec((ny, 1, 2, rows), lambda j, z: (0, j, 0, 0)),
            ],
            out_specs=[
                pl.BlockSpec((1, wide, rows), lambda j, z: (j, 0, 0)),
                pl.BlockSpec((nz, rows, wide), lambda j, z: (0, 0, 0)),
            ],
            scratch_shapes=[
                pltpu.VMEM((nz, rows, dim), jnp.float32),
                pltpu.VMEM((nz, rows, dim), jnp.float32),
            ],
        ),
        out_shape=[
            jax.ShapeDtypeStruct((ny, wide, rows), jnp.bfloat16),
            jax.ShapeDtypeStruct((nz, rows, wide), jnp.bfloat16),
        ],
        cost_estimate=pl.CostEstimate(flops=flops, transcendentals=0, bytes_accessed=8 << 20),
        name="attend_back",
    )(zh, qd, kv, p, o, st, all_st)


def to_all(x, axis, count):
    return lax.all_to_all(jnp.broadcast_to(x[None], (count,) + x.shape), axis, 0, 0, tiled=True)


def on_device(queries, key_rows, values, out_grad, query_gain, key_gain, stretch_id):
    rows, dim = queries.shape
    nz, ny = lax.axis_size("z_hi"), lax.axis_size("y")
    ns = lax.axis_size("z_lo") * lax.axis_size("x") * lax.axis_size("core")
    width = dim * ns
    zh = lax.axis_index("z_hi").astype(jnp.int32).reshape(1)
    query_wide = queries.astype(jnp.float32)
    key_wide = key_rows.astype(jnp.float32)
    squares = jnp.stack([jnp.sum(query_wide * query_wide, axis=1), jnp.sum(key_wide * key_wide, axis=1)])
    squares = jnp.sum(to_all(squares, SECTION, ns), axis=0)
    roots = lax.rsqrt(squares / width + EPSILON)
    query_root, key_root = roots[0], roots[1]
    query_hat = (query_wide * query_root[:, None] * query_gain[None, :]).astype(jnp.bfloat16)
    key_hat = (key_wide * key_root[:, None] * key_gain[None, :]).astype(jnp.bfloat16)
    sid_row = jnp.broadcast_to(stretch_id.astype(jnp.bfloat16)[None, :], (EXTRA, rows))
    packed = jnp.concatenate([jnp.concatenate([query_hat, out_grad], axis=1), sid_row], axis=0)
    qd = to_all(packed, "y", ny)
    kv = lax.all_gather(jnp.concatenate([key_hat, values], axis=1), "z_hi", axis=0)
    sid = jnp.broadcast_to(stretch_id.astype(jnp.float32)[:, None], (rows, 128))
    p, o, st = forward(zh, qd, kv, sid)
    all_st = to_all(st[:, :2, :], "y", ny)
    all_st = all_st.reshape(ny, ny, 2, rows)
    to_y, to_z = backward(zh, qd, kv, p, o, st, all_st)
    got_y = lax.all_to_all(to_y, "y", 0, 0, tiled=True)
    got_z = lax.all_to_all(to_z, "z_hi", 0, 0, tiled=True)
    sum_y = jnp.sum(got_y.astype(jnp.float32), axis=0)
    sum_z = jnp.sum(got_z.astype(jnp.float32), axis=0)
    attended = sum_y[:dim].T.astype(jnp.bfloat16)
    query_grad = sum_y[dim:].T
    key_grad = sum_z[:, :dim]
    value_grad = sum_z[:, dim:]
    terms = jnp.stack(
        [
            jnp.sum(query_grad * query_gain[None, :] * query_wide, axis=1),
            jnp.sum(key_grad * key_gain[None, :] * key_wide, axis=1),
        ]
    )
    terms = jnp.sum(to_all(terms, SECTION, ns), axis=0)
    grad_queries = (
        query_gain[None, :] * query_root[:, None] * query_grad
        - query_wide * (query_root**3 * terms[0] / width)[:, None]
    )
    grad_keys = (
        key_gain[None, :] * key_root[:, None] * key_grad
        - key_wide * (key_root**3 * terms[1] / width)[:, None]
    )
    return (attended, grad_queries, grad_keys, value_grad)


def solution(mesh):
    fine = Mesh(mesh.devices.reshape(3, 4, 2, 4, 8), SECTION + SEQ)
    full = P(SEQ, SECTION)
    return jax.shard_map(
        on_device,
        mesh=fine,
        in_specs=(full, full, full, full, P(SECTION), P(SECTION), P(SEQ)),
        out_specs=(full, full, full, full),
        check_vma=False,
    )
```
